256 devices in a mesh: expert: 64 (over z_hi, y, x, core), hidden: 4 (over z_lo).
Axes of the slice: x: 4, y: 4, z: 8 (z_hi: 2, z_lo: 4; z = z_hi * 4 + z_lo), core: 2. Of those that a mesh axis runs over, the one named last changes fastest.
Arguments:
- cotangent: bfloat16 [65536, 2048], P(('expert', 'hidden')), may hold values from -6 to 6
- slot_token: int32 [256, 64, 10], P(('expert', 'hidden')), may hold values from -1 to 255, as said below
- slot_gate: float32 [256, 64, 10], P(('expert', 'hidden')), may hold values from 0.1 to 1
- w_down: bfloat16 [64, 4096, 2048], P('expert', 'hidden'), may hold values from -0.09375 to 0.09375
Outputs:
- hidden_grad: bfloat16 [64, 2048, 4096], P('expert', None, 'hidden')
The draws below stay inside these ranges and needn't reach their ends.
Inputs may be any that keep to these rules, and one draw needn't show every extreme that they name: `slot_token`: on each device and for each expert the live slots come first and name distinct local tokens; a device fills at most 10 slots for one expert. For each expert and each index of the hidden axis, the 64 devices with that index name exactly 512 tokens together, so each expert takes exactly 2048 tokens.
All inputs are finite; a program needn't handle non-finite values.
Results may differ from the reference program's by a relative error of at most 0.0049.
Values may be sent and summed in bfloat16 or wider, within the bound.
No kernel may reach another device: no remote copies, remote signals or barrier semaphores. Data moves between devices by JAX's collectives and lax.ppermute only.
A program may use at most 128 MiB of HBM per device.

```python
import jax
import jax.numpy as jnp
from jax import lax

D = 2048
F = 4096
TOK_DEV = 256
EXPERTS = 64
SOURCES = 256
TOKENS = 65536
MEAN = 8
SLOT = 10
CAP = 2048
N_EXPERT = 64
N_HIDDEN = 4


def draw_slot_token(key, part):
    groups = N_HIDDEN
    sources = N_EXPERT
    half_count = sources // 2
    spread = MEAN // 4
    key_order = jax.random.fold_in(key, 11)
    key_shift = jax.random.fold_in(key, 12)
    key_token = jax.random.fold_in(key, 13)
    scores = jax.random.randint(key_order, (EXPERTS, groups, sources), 0, 1 << 20) * sources + jnp.arange(sources, dtype=jnp.int32)
    ranking = jnp.argsort(scores, axis=-1).astype(jnp.int32)
    shifts = jax.random.randint(key_shift, (EXPERTS, groups, half_count), -spread, spread + 1)
    shifts = jnp.where(jnp.arange(half_count)[None, None, :] == 0, spread, shifts)
    by_rank = MEAN + jnp.concatenate([shifts, -shifts], axis=-1)
    inverse = jnp.argsort(ranking, axis=-1).astype(jnp.int32)
    per_source = jnp.take_along_axis(by_rank, inverse, axis=-1)
    per_device = jnp.transpose(per_source, (2, 1, 0)).reshape(SOURCES, EXPERTS)
    token_scores = jax.random.randint(key_token, (SOURCES, EXPERTS, TOK_DEV), 0, 1 << 20) * TOK_DEV + jnp.arange(TOK_DEV, dtype=jnp.int32)
    chosen = jnp.argsort(token_scores, axis=-1)[:, :, :SLOT].astype(jnp.int32)
    live_slot = jnp.arange(SLOT, dtype=jnp.int32)[None, None, :] < per_device[:, :, None]
    return jnp.where(live_slot, chosen, -1).astype(jnp.int32)


def block_scale(rng, extent, cuts, least, high):
    def one(axis_at, shards_of):
        steps = jax.random.uniform(jax.random.fold_in(jax.random.fold_in(rng, 6), axis_at), (shards_of,), jnp.float32, least / len(cuts), high / len(cuts))
        return jnp.repeat(jnp.exp(steps), extent[axis_at] // shards_of).reshape((-1,) + (1,) * (len(extent) - axis_at - 1))

    factor_of = one(*cuts[0])
    for cut in cuts[1:]:
        factor_of = factor_of * one(*cut)
    return factor_of


def noise(stream_key, shape, scale, bound, pieces=(), kind=jnp.bfloat16):
    level = block_scale(stream_key, shape, pieces, -0.22, 0.18) if pieces else 1.0
    result = jax.random.normal(stream_key, shape, jnp.float32) * scale * level
    return jnp.minimum(jnp.maximum(result, -bound), bound).astype(kind)


def setup_inputs(seed: int = 0) -> dict:
    arg_keys = jax.random.split(jax.random.key(seed), 5)
    cotangent = noise(arg_keys[0], (TOKENS, D), 1.0, 6.0, ((0, 256),))
    slot_token = draw_slot_token(jax.random.fold_in(arg_keys[4], 71), 0)
    slot_gate = jnp.clip(0.1 + 0.9 * jax.random.uniform(arg_keys[2], (SOURCES, EXPERTS, SLOT), jnp.float32) ** block_scale(arg_keys[2], (SOURCES, EXPERTS, SLOT), ((0, 256),), -0.2, 0.2), 0.1, 1.0)
    w_down = noise(arg_keys[3], (EXPERTS, F, D), F ** -0.5, 0.09375, ((0, 64), (1, 4)))
    return {"cotangent": cotangent, "slot_token": slot_token, "slot_gate": slot_gate, "w_down": w_down}


def reference(cotangent, slot_token, slot_gate, w_down):
    live_slot = slot_token >= 0
    row_base = (jnp.arange(SOURCES, dtype=jnp.int32) * TOK_DEV)[:, None, None]
    token_id = (row_base + jnp.maximum(slot_token, 0)).astype(jnp.int32)
    gate_value = jnp.where(live_slot, slot_gate, jnp.float32(0.0))
    slot_count = jnp.sum(live_slot.astype(jnp.int32), axis=2)

    def reorder(values):
        shaped = values.reshape((N_EXPERT, N_HIDDEN) + values.shape[1:])
        moved = jnp.moveaxis(jnp.moveaxis(shaped, 2, 0), 2, 1)
        return moved.reshape((EXPERTS, SOURCES) + values.shape[2:])

    token_order = reorder(token_id)
    gate_order = reorder(gate_value)
    count_order = reorder(slot_count[:, :, None])[:, :, 0]

    def one_expert(items):
        token_rows, gate_rows, count_rows, weight = items
        picked = cotangent[token_rows.reshape(-1)]
        scaled = (gate_rows.reshape(-1)[:, None] * picked.astype(jnp.float32)).astype(jnp.bfloat16)
        running = jnp.cumsum(count_rows).astype(jnp.int32)
        first_slot = running - count_rows
        row_number = jnp.arange(CAP, dtype=jnp.int32)
        source = jnp.sum((running[None, :] <= row_number[:, None]).astype(jnp.int32), axis=1).astype(jnp.int32)
        flat_index = (source * SLOT + row_number - first_slot[source]).astype(jnp.int32)
        routed = scaled[flat_index]
        return jnp.dot(routed, weight.T, preferred_element_type=jnp.float32).astype(jnp.bfloat16)

    return lax.map(one_expert, (token_order, gate_order, count_order, w_down))
```

```python
import jax
import jax.numpy as jnp
from jax import lax
from jax.sharding import Mesh, PartitionSpec as P

AXES = ("zhi", "y", "x", "core", "zlo")
COLUMN = ("zhi", "zlo")
PLANE = ("y", "x", "core")
CHUNKS = (512, 512, 512, 512)
DEAD = 128.0


def shards(cotangent, slot_token, slot_gate, w_down):
    tokens, features = cotangent.shape
    experts, width = slot_token.shape[1:]
    planes = 8
    half = experts // 2
    rows = half * planes * width
    hidden = w_down.shape[1]

    table = jnp.concatenate([slot_token.astype(jnp.float32).reshape(1, -1), slot_gate.reshape(1, -1)], axis=1)
    table = lax.all_gather(table, COLUMN, axis=0, tiled=True).reshape(planes, 2, experts, width)
    table = lax.dynamic_slice_in_dim(table, lax.axis_index("zhi") * half, half, axis=2)
    slot = jnp.transpose(table[:, 0], (1, 0, 2)).astype(jnp.int32)
    gate = jnp.transpose(table[:, 1], (1, 0, 2)).reshape(rows, 1)
    live = (slot >= 0).reshape(rows, 1)
    row = (slot + tokens * jnp.arange(planes, dtype=jnp.int32)[None, :, None]).reshape(rows, 1)
    row = jnp.where(live, row, -1)
    pick = (row == jnp.arange(planes * tokens, dtype=jnp.int32)[None, :]).astype(jnp.bfloat16)

    total = None
    place = None
    start = 0
    for chunk in CHUNKS:
        part = lax.all_gather(cotangent[:, start : start + chunk], COLUMN, axis=0, tiled=True)
        picked = jnp.dot(pick, part, preferred_element_type=jnp.float32)
        scaled = jnp.where(live, gate * picked, DEAD).astype(jnp.bfloat16)
        arrived = lax.all_to_all(scaled, PLANE, split_axis=0, concat_axis=0, tiled=True)
        if place is None:
            alive = (arrived[:, 0] < 64.0).astype(jnp.int32).reshape(half, 2, 4, width)
            alive = jnp.transpose(alive, (2, 1, 0, 3)).reshape(-1)
            at = jnp.where(alive > 0, jnp.cumsum(alive) - 1, -1)
            at = jnp.transpose(at.reshape(4, 2, half, width), (2, 1, 0, 3)).reshape(1, rows)
            place = (at == jnp.arange(planes * tokens, dtype=jnp.int32)[:, None]).astype(jnp.bfloat16)
        term = lax.dot_general(
            arrived, w_down[0, :, start : start + chunk], (((1,), (1,)), ((), ())), preferred_element_type=jnp.float32
        )
        total = term if total is None else total + term
        start += chunk
    result = jnp.dot(place, total.astype(jnp.bfloat16), preferred_element_type=jnp.float32)
    return result.astype(jnp.bfloat16)[None]


def solution(mesh):
    fine = Mesh(mesh.devices.reshape(2, 4, 4, 2, 4), AXES)
    wide = ("zhi", "y", "x", "core")
    in_specs = (P(AXES, None), P(AXES, None, None), P(AXES, None, None), P(wide, "zlo", None))
    return jax.shard_map(shards, mesh=fine, in_specs=in_specs, out_specs=P(wide, None, "zlo"), check_vma=False)
```

```python
import functools

import jax
import jax.numpy as jnp
from jax import lax
from jax.experimental import pallas as pl
from jax.experimental.pallas import tpu as pltpu
from jax.sharding import Mesh, PartitionSpec as P


AXES = ("zhi", "y", "x", "core", "zlo")
COLUMN = ("zhi", "zlo")
PLANE = ("y", "x", "core")
PLANES = 8
DEAD = 128.0
HEAD = 8
UP = [(i, (i + 1) % PLANES) for i in range(PLANES)]
DOWN = [(i, (i - 1) % PLANES) for i in range(PLANES)]
GROUPS = (((0,), 4), ((-1, 1), 2), ((-2, 2), 2), ((-3, 3, 4), 1))
TILES = 4
SKIP = 8192
CONTRACT_LAST = (((1,), (1,)), ((), ()))


def ring(a, b):
    return lax.ppermute(a, COLUMN, UP), lax.ppermute(b, COLUMN, DOWN)


def pack_table(slot_token, slot_gate, columns):
    gate = slot_gate.reshape(1, -1)
    high = lax.reduce_precision(gate, 8, 7)
    middle = lax.reduce_precision(gate - high, 8, 7)
    low = gate - high - middle
    table = jnp.concatenate([slot_token.astype(jnp.float32).reshape(1, -1), high, middle, low], axis=0)
    return jnp.pad(table, ((0, HEAD - 4), (0, columns - table.shape[1]))).astype(jnp.bfloat16)


def dispatch_kernel(sources, pieces, half, width, padded, zhi_ref, *refs):
    out_ref = refs[-1]
    parts = refs[:-1]
    columns = out_ref.shape[1]
    each = half // TILES
    rows = each * padded
    slots = 2 * half * width
    whole = sources if len(parts) == sources else sources - 1
    tables = [parts[j][parts[j].shape[0] - HEAD :, :slots] for j in range(sources)]
    first = zhi_ref[0] * half + pl.program_id(0) * each

    def block_of(rem):
        block = jnp.zeros_like(rem)
        for i in range(1, sources * pieces):
            block = block + (rem >= i * width).astype(jnp.int32)
        return block

    shape = (each, padded, slots)
    rem = lax.broadcasted_iota(jnp.int32, shape, 1)
    block = block_of(rem)
    target = (first + lax.broadcasted_iota(jnp.int32, shape, 0)) * width + rem - block * width
    hit = lax.broadcasted_iota(jnp.int32, shape, 2) == target
    data = jnp.zeros((rows, HEAD), jnp.float32)
    for j in range(sources):
        mine = hit & (block >= j * pieces) & (block < (j + 1) * pieces)
        mine = jnp.where(mine, 1.0, 0.0).reshape(rows, slots).astype(jnp.bfloat16)
        data = data + lax.dot_general(mine, tables[j], CONTRACT_LAST, preferred_element_type=jnp.float32)
    token = data[:, 0:1]
    gate = data[:, 1:2] + data[:, 2:3] + data[:, 3:4]
    rem = lax.broadcasted_iota(jnp.int32, (each, padded, 1), 1).reshape(rows, 1)
    block = block_of(rem)
    token = jnp.where(rem < sources * pieces * width, token, -1.0)
    total = None
    for j in range(sources):
        for q in range(pieces):
            token_of = jnp.where(block == j * pieces + q, token, -1.0)
            if j < whole:
                spans = [(parts[j], 0, parts[j].shape[0] - HEAD)]
            else:
                low = parts[-1].shape[0]
                spans = [(parts[-1], 0, low), (parts[j], low, parts[j].shape[0] - HEAD)]
            for ref, base, length in spans:
                lane = lax.broadcasted_iota(jnp.int32, (rows, length), 1).astype(jnp.float32) + float(base)
                pick = jnp.where(lane == token_of, 1.0, 0.0).astype(jnp.bfloat16)
                term = jnp.dot(
                    pick, ref[:length, q * columns : (q + 1) * columns], preferred_element_type=jnp.float32
                )
                total = term if total is None else total + term
    out_ref[...] = jnp.where(token >= 0.0, gate * total, DEAD).astype(jnp.bfloat16)


def dispatch(number, zhi, parts, half, width):
    sources, pieces = GROUPS[number]
    columns = parts[0].shape[1] // pieces
    used = len(sources) * pieces * width
    padded = -(-used // 8) * 8
    rows = half * padded
    depth = sum(p.shape[0] for p in parts)
    return pl.pallas_call(
        functools.partial(dispatch_kernel, len(sources), pieces, half, width, padded),
        grid_spec=pltpu.PrefetchScalarGridSpec(
            num_scalar_prefetch=1,
            grid=(TILES,),
            in_specs=[pl.BlockSpec(p.shape, lambda t, s: (0, 0)) for p in parts],
            out_specs=pl.BlockSpec((rows // TILES, columns), lambda t, s: (t, 0)),
        ),
        out_shape=jax.ShapeDtypeStruct((rows, columns), jnp.bfloat16),
        cost_estimate=pl.CostEstimate(
            flops=2 * rows * depth * columns, bytes_accessed=2 * (depth * pieces + rows) * columns, transcendentals=0
        ),
    )(zhi.reshape(1), *parts)


def places(x_ref, sources, pieces, half, width, share, z):
    rows = x_ref.shape[0]
    padded = rows // half
    first = jnp.where(lax.broadcasted_iota(jnp.int32, (8, 128), 1) == 0, 1.0, 0.0).astype(jnp.bfloat16)
    value = lax.dot_general(first, x_ref[:, :128], CONTRACT_LAST, preferred_element_type=jnp.float32)

    def block_of(shape, axis):
        index = lax.broadcasted_iota(jnp.int32, shape, axis).astype(jnp.float32)
        place = jnp.floor((index + 0.5) * (1.0 / padded))
        return index, jnp.floor((index - place * padded + 0.5) * (1.0 / width))

    index, block = block_of((1, rows), 1)
    index_down, block_down = block_of((rows, 1), 0)
    alive = jnp.where((value < 64.0) & (block < len(sources) * pieces), 1.0, 0.0)
    earlier = jnp.where((block_down == block) & (index_down < index), 1.0, 0.0).astype(jnp.bfloat16)
    code = jnp.dot(alive.astype(jnp.bfloat16), earlier, preferred_element_type=jnp.float32)
    for j, offset in enumerate(sources):
        source = lax.rem(z + (offset + PLANES), PLANES)
        held = jnp.sum(jnp.where(block == j * pieces, alive[0:1], 0.0), axis=1, keepdims=True)
        upper = jnp.where(source >= 4, 1.0, 0.0)
        base = (lax.rem(source, 4) * share).astype(jnp.float32) + upper * (share - held)
        for q in range(pieces):
            code = code + jnp.where(block == j * pieces + q, base + float(SKIP * q), 0.0)
    return jnp.where(alive > 0.0, code, -1.0).astype(jnp.int32)


def chosen(code, share, h, q):
    position = lax.broadcasted_iota(jnp.int32, (share, code.shape[1]), 0) + (h * share + SKIP * q)
    return jnp.where(code == position, 1.0, 0.0).astype(jnp.bfloat16)


def early_kernel(half, width, s_ref, x0_ref, x1_ref, x2_ref, w_ref, out_ref, row_ref, c0_ref, c1_ref):
    i = pl.program_id(0)
    share = out_ref.shape[0]
    h = s_ref[1 + i]

    def route(number, x_ref, c_ref, fresh):
        sources, pieces = GROUPS[number]

        @pl.when(fresh)
        def _():
            c_ref[...] = places(x_ref, sources, pieces, half, width, share, s_ref[0])

        columns = x_ref.shape[1]
        for q in range(pieces):
            row_ref[:, q * columns : (q + 1) * columns] = jnp.dot(
                chosen(c_ref[0:1, :], share, h, q), x_ref[...], preferred_element_type=jnp.float32
            ).astype(jnp.bfloat16)

    @pl.when(i == 0)
    def _():
        route(0, x0_ref, c0_ref, i == 0)

    @pl.when((i == 1) | (i == 2))
    def _():
        route(1, x1_ref, c1_ref, i == 1)

    @pl.when(i == 3)
    def _():
        route(2, x2_ref, c0_ref, i == 3)

    out_ref[...] = lax.dot_general(
        row_ref[...], w_ref[...], CONTRACT_LAST, preferred_element_type=jnp.float32
    ).astype(jnp.bfloat16)


def early(z, x0, x1, x2, weight, half, width, share):
    hidden, features = weight.shape
    rows = x1.shape[0]
    order = jnp.stack([z, z % 4, (z - 1) % 4, (z + 1) % 4, (z + 2) % 4])
    return pl.pallas_call(
        functools.partial(early_kernel, half, width),
        grid_spec=pltpu.PrefetchScalarGridSpec(
            num_scalar_prefetch=1,
            grid=(4,),
            in_specs=[pl.BlockSpec(a.shape, lambda i, s: (0, 0)) for a in (x0, x1, x2, weight)],
            out_specs=pl.BlockSpec((share, hidden), lambda i, s: (s[1 + i], 0)),
            scratch_shapes=[
                pltpu.VMEM((share, features), jnp.bfloat16),
                pltpu.VMEM((8, rows), jnp.int32),
                pltpu.VMEM((8, rows), jnp.int32),
            ],
        ),
        out_shape=jax.ShapeDtypeStruct((4 * share, hidden), jnp.bfloat16),
        name="early",
        cost_estimate=pl.CostEstimate(
            flops=8 * share * features * (rows + hidden), bytes_accessed=4 * features * (rows + hidden), transcendentals=0
        ),
        compiler_params=pltpu.CompilerParams(vmem_limit_bytes=56 << 20),
    )(order, x0, x1, x2, weight)


def late_kernel(half, width, steps, s_ref, front_ref, x_ref, w_ref, old_ref, out_ref, c_ref, y_ref):
    i = pl.program_id(0)
    share = out_ref.shape[0]
    tile = x_ref.shape[0]

    @pl.when(i == 0)
    def _():
        c_ref[...] = places(front_ref, GROUPS[3][0], 1, half, width, share, s_ref[0])

    @pl.when(i < steps)
    def _():
        y_ref[pl.ds(pl.multiple_of(i * tile, 16), tile), :] = lax.dot_general(
            x_ref[...], w_ref[...], CONTRACT_LAST, preferred_element_type=jnp.float32
        ).astype(jnp.bfloat16)

    @pl.when(i >= steps)
    def _():
        h = s_ref[1 + jnp.maximum(i - steps, 0)]
        out = jnp.dot(chosen(c_ref[0:1, :], share, h, 0), y_ref[...], preferred_element_type=jnp.float32)
        out_ref[...] = (out + old_ref[...].astype(jnp.float32)).astype(jnp.bfloat16)


def late(z, x, weight, old, half, width, share):
    hidden, features = weight.shape
    rows = x.shape[0]
    steps = 4
    order = jnp.stack([z] + [(z + offset) % 4 for offset in GROUPS[3][0]])
    count = len(GROUPS[3][0])
    tile = pl.BlockSpec((share, hidden), lambda i, s: (s[1 + jnp.maximum(i - steps, 0)], 0))
    return pl.pallas_call(
        functools.partial(late_kernel, half, width, steps),
        grid_spec=pltpu.PrefetchScalarGridSpec(
            num_scalar_prefetch=1,
            grid=(steps + count,),
            in_specs=[
                pl.BlockSpec((rows, 128), lambda i, s: (0, 0)),
                pl.BlockSpec((rows // steps, features), lambda i, s: (jnp.minimum(i, steps - 1), 0)),
                pl.BlockSpec((hidden, features), lambda i, s: (0, 0)),
                tile,
            ],
            out_specs=tile,
            scratch_shapes=[pltpu.VMEM((8, rows), jnp.int32), pltpu.VMEM((rows, hidden), jnp.bfloat16)],
        ),
        out_shape=jax.ShapeDtypeStruct((4 * share, hidden), jnp.bfloat16),
        input_output_aliases={4: 0},
        name="late",
        cost_estimate=pl.CostEstimate(
            flops=2 * rows * hidden * (features + share * count),
            bytes_accessed=2 * features * (rows + hidden) + 4 * share * count * hidden,
            transcendentals=0,
        ),
        compiler_params=pltpu.CompilerParams(vmem_limit_bytes=56 << 20),
    )(order, x, x, weight, old)


def hold_kernel(a_ref, o_ref):
    o_ref[...] = a_ref[...]


def hold(a):
    a = a[:8, :128]
    return pl.pallas_call(
        hold_kernel,
        out_shape=jax.ShapeDtypeStruct(a.shape, a.dtype),
        compiler_params=pltpu.CompilerParams(has_side_effects=True),
    )(a)


def shards(cotangent, slot_token, slot_gate, w_down):
    tokens, features = cotangent.shape
    experts, width = slot_token.shape[1:]
    half = experts // 2
    mid = tokens // 2
    share = 2 * tokens
    weight = w_down[0]
    zhi = lax.axis_index("zhi")
    z = zhi * 4 + lax.axis_index("zlo")

    def send(number, parts):
        scaled = dispatch(number, zhi, parts, half, width)
        return scaled, lax.all_to_all(scaled, PLANE, split_axis=0, concat_axis=0, tiled=True)

    own = jnp.concatenate([cotangent, pack_table(slot_token, slot_gate, features)], axis=0)
    u1, d1 = ring(own, own)
    _, x0 = send(0, [own])
    u2, d2 = ring(u1, d1)
    _, x1 = send(1, [u1, d1])
    hold(x0)
    u3, d3 = ring(u2, d2)
    _, x2 = send(2, [u2, d2])
    hold(x1)
    u4, d4 = ring(u3[mid:], d3[:mid])
    _, x3 = send(3, [u3, d3, u4, d4])

    out = early(z, x0, x1, x2, weight, half, width, share)
    out = late(z, x3, weight, out, half, width, share)
    return out[None]


def solution(mesh):
    fine = Mesh(mesh.devices.reshape(2, 4, 4, 2, 4), AXES)
    wide = ("zhi", "y", "x", "core")
    in_specs = (P(AXES, None), P(AXES, None, None), P(AXES, None, None), P(wide, "zlo", None))
    return jax.shard_map(shards, mesh=fine, in_specs=in_specs, out_specs=P(wide, None, "zlo"), check_vma=False)
```

```python
import functools

import jax
import jax.numpy as jnp
from jax import lax
from jax.experimental import pallas as pl
from jax.experimental.pallas import tpu as pltpu
from jax.sharding import Mesh, PartitionSpec as P


AXES = ("zhi", "y", "x", "core", "zlo")
COLUMN = ("zhi", "zlo")
PLANE = ("y", "x", "core")
PLANES = 8
DEAD = 128.0
HEAD = 8
UP = [(i, (i + 1) % PLANES) for i in range(PLANES)]
SWAP = [(i, i ^ 1) for i in range(PLANES)]
DOWN = [(i, (i - 1) % PLANES) for i in range(PLANES)]
GROUPS = ((1, 4), (1, 4), (2, 2), (3, 1))
TILES = 4
SKIP = 8192
CONTRACT_LAST = (((1,), (1,)), ((), ()))


def ring(a, b):
    return lax.ppermute(a, COLUMN, UP), lax.ppermute(b, COLUMN, DOWN)


def pack_table(slot_token, slot_gate, columns):
    gate = slot_gate.reshape(1, -1)
    high = lax.reduce_precision(gate, 8, 7)
    middle = lax.reduce_precision(gate - high, 8, 7)
    low = gate - high - middle
    table = jnp.concatenate([slot_token.astype(jnp.float32).reshape(1, -1), high, middle, low], axis=0)
    return jnp.pad(table, ((0, HEAD - 4), (0, columns - table.shape[1]))).astype(jnp.bfloat16)


def dispatch_kernel(number, half, width, padded, s_ref, *refs):
    *parts, out_ref, stack_ref, table_ref = refs
    sources, pieces = GROUPS[number]
    columns = out_ref.shape[1]
    each = half // TILES
    rows = each * padded
    depth = stack_ref.shape[0]
    tokens = depth // (sources * pieces)
    slots = table_ref.shape[2]
    t = pl.program_id(0)

    def load(j, ref, base, length, table=True):
        for q in range(pieces):
            to = (j * pieces + q) * tokens + base
            stack_ref[to : to + length, :] = ref[:length, q * columns : (q + 1) * columns]
        if table:
            table_ref[j] = ref[length : length + HEAD, :slots]

    if number == 1:
        pl.when((t == 0) & (s_ref[1] == 0))(functools.partial(load, 0, parts[0], 0, tokens))
        pl.when((t == 0) & (s_ref[1] == 1))(functools.partial(load, 0, parts[1], 0, tokens))
    else:

        @pl.when(t == 0)
        def _():
            for j in range(min(sources, 2)):
                load(j, parts[j], 0, tokens)
            if number == 3:
                mid = tokens // 2
                load(2, parts[2], mid, mid)
                load(2, parts[3], 0, mid, table=False)

    first = s_ref[0] * half + t * each
    index = lax.broadcasted_iota(jnp.int32, (rows, 1), 0).astype(jnp.float32)
    place = jnp.floor((index + 0.5) * (1.0 / padded))
    rem = index - place * padded
    block = jnp.floor((rem + 0.5) * (1.0 / width))
    target = (first.astype(jnp.float32) + place) * width + rem - block * width
    lane = lax.broadcasted_iota(jnp.int32, (rows, slots), 1)
    data = jnp.zeros((rows, HEAD), jnp.float32)
    for j in range(sources):
        mine = (block >= j * pieces) & (block < (j + 1) * pieces)
        mine = jnp.where(mine, target, -1.0).astype(jnp.int32)
        mine = jnp.where(lane == mine, 1.0, 0.0).astype(jnp.bfloat16)
        data = data + lax.dot_general(mine, table_ref[j], CONTRACT_LAST, preferred_element_type=jnp.float32)
    token = data[:, 0:1]
    gate = data[:, 1:2] + data[:, 2:3] + data[:, 3:4]
    goal = jnp.where((token >= 0.0) & (block < sources * pieces), token + block * tokens, -1.0).astype(jnp.int32)
    lane = lax.broadcasted_iota(jnp.int32, (rows, depth), 1)
    pick = jnp.where(lane == goal, 1.0, 0.0).astype(jnp.bfloat16)
    total = jnp.dot(pick, stack_ref[...], preferred_element_type=jnp.float32)
    out_ref[...] = jnp.where(goal >= 0, gate * total, DEAD).astype(jnp.bfloat16)


def dispatch(number, scalars, parts, tokens, half, width):
    sources, pieces = GROUPS[number]
    columns = parts[0].shape[1] // pieces
    used = sources * pieces * width
    padded = -(-used // 8) * 8
    rows = half * padded
    depth = sources * pieces * tokens
    return pl.pallas_call(
        functools.partial(dispatch_kernel, number, half, width, padded),
        grid_spec=pltpu.PrefetchScalarGridSpec(
            num_scalar_prefetch=1,
            grid=(TILES,),
            in_specs=[pl.BlockSpec(p.shape, lambda t, s: (0, 0)) for p in parts],
            out_specs=pl.BlockSpec((rows // TILES, columns), lambda t, s: (t, 0)),
            scratch_shapes=[
                pltpu.VMEM((depth, columns), jnp.bfloat16),
                pltpu.VMEM((sources, HEAD, 2 * half * width), jnp.bfloat16),
            ],
        ),
        out_shape=jax.ShapeDtypeStruct((rows, columns), jnp.bfloat16),
        cost_estimate=pl.CostEstimate(
            flops=2 * rows * depth * columns, bytes_accessed=2 * (depth + rows) * columns, transcendentals=0
        ),
    )(scalars, *parts)


def places(x_ref, sources, pieces, half, width, share):
    rows = x_ref.shape[0]
    padded = rows // half
    first = jnp.where(lax.broadcasted_iota(jnp.int32, (8, 128), 1) == 0, 1.0, 0.0).astype(jnp.bfloat16)
    value = lax.dot_general(first, x_ref[:, :128], CONTRACT_LAST, preferred_element_type=jnp.float32)

    def split(index, length):
        outer = jnp.floor((index + 0.5) * (1.0 / length))
        return outer, index - outer * length

    def parts(shape, axis):
        place, rem = split(lax.broadcasted_iota(jnp.int32, shape, axis).astype(jnp.float32), padded)
        block, slot = split(rem, width)
        source, piece = split(block, pieces)
        return place, block, slot, source, piece

    place, block, slot, source, piece = parts((1, rows), 1)
    alive = jnp.where((value < 64.0) & (block < len(sources) * pieces), 1.0, 0.0)
    place_down, _, _, source_down, piece_down = parts((rows, 1), 0)
    lane = lax.broadcasted_iota(jnp.int32, (rows, 128), 1)
    own = jnp.where(piece_down == 0.0, source_down * half + place_down, -1.0).astype(jnp.int32)
    own = jnp.where(lane == own, 1.0, 0.0).astype(jnp.bfloat16)
    count = jnp.dot(alive.astype(jnp.bfloat16), own, preferred_element_type=jnp.float32)
    of, at = split(lax.broadcasted_iota(jnp.int32, (128, 1), 0).astype(jnp.float32), half)
    ahead = jnp.where((of == source) & (at < place), 1.0, 0.0).astype(jnp.bfloat16)
    code = jnp.dot(count.astype(jnp.bfloat16), ahead, preferred_element_type=jnp.float32)
    code = code + slot + piece * float(SKIP)
    of, _ = split(lax.broadcasted_iota(jnp.int32, (1, 128), 1).astype(jnp.float32), half)
    for j, z in enumerate(sources):
        held = jnp.sum(jnp.where(of == j, count[0:1], 0.0), axis=1, keepdims=True)
        upper = jnp.where(z >= 4, 1.0, 0.0)
        base = (lax.rem(z, 4) * share).astype(jnp.float32) + upper * (share - held)
        code = code + jnp.where(source == j, base, 0.0)
    return jnp.where(alive > 0.0, code, -1.0).astype(jnp.int32)


def chosen(code, share, h, q):
    position = lax.broadcasted_iota(jnp.int32, (share, code.shape[1]), 0) + (h * share + SKIP * q)
    return jnp.where(code == position, 1.0, 0.0).astype(jnp.bfloat16)


def early_kernel(half, width, s_ref, x0_ref, xp_ref, x1_ref, x2_ref, w_ref, out_ref, row_ref, c_ref):
    i = pl.program_id(0)
    share = out_ref.shape[0]
    h = s_ref[i]

    def route(x_ref, sources, pieces):
        c_ref[...] = places(x_ref, sources, pieces, half, width, share)
        columns = x_ref.shape[1]
        for q in range(pieces):
            row_ref[:, q * columns : (q + 1) * columns] = jnp.dot(
                chosen(c_ref[0:1, :], share, h, q), x_ref[...], preferred_element_type=jnp.float32
            ).astype(jnp.bfloat16)

    for step, x_ref in enumerate((x0_ref, xp_ref, x1_ref)):
        pl.when(i == step)(functools.partial(route, x_ref, [s_ref[4 + step]], 4))
    pl.when(i == 3)(functools.partial(route, x2_ref, [s_ref[7], s_ref[8]], 2))

    out_ref[...] = lax.dot_general(
        row_ref[...], w_ref[...], CONTRACT_LAST, preferred_element_type=jnp.float32
    ).astype(jnp.bfloat16)


def early(sources, arrived, weight, half, width, share):
    hidden, features = weight.shape
    rows = arrived[0].shape[0]
    order = jnp.stack([s % 4 for s in sources[:4]] + sources)
    return pl.pallas_call(
        functools.partial(early_kernel, half, width),
        grid_spec=pltpu.PrefetchScalarGridSpec(
            num_scalar_prefetch=1,
            grid=(4,),
            in_specs=[pl.BlockSpec(a.shape, lambda i, s: (0, 0)) for a in (*arrived, weight)],
            out_specs=pl.BlockSpec((share, hidden), lambda i, s: (s[i], 0)),
            scratch_shapes=[
                pltpu.VMEM((share, features), jnp.bfloat16),
                pltpu.VMEM((8, rows), jnp.int32),
            ],
        ),
        out_shape=jax.ShapeDtypeStruct((4 * share, hidden), jnp.bfloat16),
        name="early",
        cost_estimate=pl.CostEstimate(
            flops=8 * share * features * (rows + hidden), bytes_accessed=4 * features * (rows + hidden), transcendentals=0
        ),
        compiler_params=pltpu.CompilerParams(vmem_limit_bytes=56 << 20),
    )(order, *arrived, weight)


def late_kernel(half, width, steps, s_ref, front_ref, x_ref, w_ref, old_ref, out_ref, c_ref, y_ref, p_ref):
    i = pl.program_id(0)
    share = out_ref.shape[0]
    tile = x_ref.shape[0]

    @pl.when(i == 0)
    def _():
        c_ref[...] = places(front_ref, [s_ref[3], s_ref[4], s_ref[5]], 1, half, width, share)

    def multiply():
        y_ref[pl.ds(pl.multiple_of(i * tile, 16), tile), :] = lax.dot_general(
            x_ref[...], w_ref[...], CONTRACT_LAST, preferred_element_type=jnp.float32
        ).astype(jnp.bfloat16)

    pl.when(i == 0)(multiply)

    @pl.when((i > 0) & (i < steps))
    def _():
        multiply()
        p_ref[i - 1] = chosen(c_ref[0:1, :], share, s_ref[i - 1], 0)

    @pl.when(i >= steps)
    def _():
        out = jnp.dot(p_ref[jnp.maximum(i - steps, 0)], y_ref[...], preferred_element_type=jnp.float32)
        out_ref[...] = (out + old_ref[...].astype(jnp.float32)).astype(jnp.bfloat16)


def late(sources, x, weight, old, half, width, share):
    hidden, features = weight.shape
    rows = x.shape[0]
    steps = 4
    order = jnp.stack([s % 4 for s in sources] + sources)
    count = len(sources)
    tile = pl.BlockSpec((share, hidden), lambda i, s: (s[jnp.maximum(i - steps, 0)], 0))
    return pl.pallas_call(
        functools.partial(late_kernel, half, width, steps),
        grid_spec=pltpu.PrefetchScalarGridSpec(
            num_scalar_prefetch=1,
            grid=(steps + count,),
            in_specs=[
                pl.BlockSpec((rows, 128), lambda i, s: (0, 0)),
                pl.BlockSpec((rows // steps, features), lambda i, s: (jnp.minimum(i, steps - 1), 0)),
                pl.BlockSpec((hidden, features), lambda i, s: (0, 0)),
                tile,
            ],
            out_specs=tile,
            scratch_shapes=[
                pltpu.VMEM((8, rows), jnp.int32),
                pltpu.VMEM((rows, hidden), jnp.bfloat16),
                pltpu.VMEM((count, share, rows), jnp.bfloat16),
            ],
        ),
        out_shape=jax.ShapeDtypeStruct((4 * share, hidden), jnp.bfloat16),
        input_output_aliases={4: 0},
        name="late",
        cost_estimate=pl.CostEstimate(
            flops=2 * rows * hidden * (features + share * count),
            bytes_accessed=2 * features * (rows + hidden) + 4 * share * count * hidden,
            transcendentals=0,
        ),
        compiler_params=pltpu.CompilerParams(vmem_limit_bytes=56 << 20),
    )(order, x, x, weight, old)


def hold_kernel(a_ref, o_ref):
    o_ref[...] = a_ref[...]


def hold(a):
    a = a[:8, :128]
    return pl.pallas_call(
        hold_kernel,
        out_shape=jax.ShapeDtypeStruct(a.shape, a.dtype),
        compiler_params=pltpu.CompilerParams(has_side_effects=True),
    )(a)


def shards(cotangent, slot_token, slot_gate, w_down):
    tokens, features = cotangent.shape
    experts, width = slot_token.shape[1:]
    half = experts // 2
    mid = tokens // 2
    share = 2 * tokens
    weight = w_down[0]
    zhi = lax.axis_index("zhi")
    z = zhi * 4 + lax.axis_index("zlo")
    odd = z % 2
    scalars = jnp.stack([zhi, odd])

    def send(number, parts):
        scaled = dispatch(number, scalars, parts, tokens, half, width)
        return scaled, lax.all_to_all(scaled, PLANE, split_axis=0, concat_axis=0, tiled=True)

    own = jnp.concatenate([cotangent, pack_table(slot_token, slot_gate, features)], axis=0)
    u1, d1 = ring(own, own)
    _, x0 = send(0, [own])
    u2, d2 = ring(u1, d1)
    _, x1 = send(1, [u1, d1])
    hold(x0)
    u3, d3 = ring(u2, d2)
    _, x2 = send(2, [u2, d2])
    hold(x1)
    u4, d4 = ring(u3[mid:], d3[:mid])
    _, x3 = send(3, [u3, d3, u4, d4])

    xp = lax.ppermute(x0, COLUMN, SWAP)

    def at(*offsets):
        return [(z + o) % PLANES for o in offsets]

    partner = z + 1 - 2 * odd
    other = (z - 1 + 2 * odd) % PLANES
    out = early([z, partner, other] + at(-2, 2), (x0, xp, x1, x2), weight, half, width, share)
    out = late(at(-3, 3, 4), x3, weight, out, half, width, share)
    return out[None]


def solution(mesh):
    fine = Mesh(mesh.devices.reshape(2, 4, 4, 2, 4), AXES)
    wide = ("zhi", "y", "x", "core")
    in_specs = (P(AXES, None), P(AXES, None, None), P(AXES, None, None), P(wide, "zlo", None))
    return jax.shard_map(shards, mesh=fine, in_specs=in_specs, out_specs=P(wide, None, "zlo"), check_vma=False)
```
